32 devices in a mesh: ctx: 4 (over z), grp: 8 (over y, x, core).
Axes of the slice: x: 2, y: 2, z: 4, core: 2. Of those that a mesh axis runs over, the one named last changes fastest.
Arguments:
- queries: bfloat16 [8, 512, 1024], P('grp', 'ctx'), may hold values from -3 to 3
- keys: bfloat16 [8, 512, 128], P('grp', 'ctx'), may hold values from -1.6953125 to 1.6953125
- values: bfloat16 [8, 512, 128], P('grp', 'ctx'), may hold values from -1.6953125 to 1.6953125
- d_out: bfloat16 [8, 512, 1024], P('grp', 'ctx'), may hold values from -6 to 6
- fwd_out: bfloat16 [8, 512, 1024], P('grp', 'ctx'), may hold values from -0.59765625 to 0.59765625
- lse: float32 [8, 8, 512], P('grp', None, 'ctx'), as said below
- segment_ids: int32 [8, 512], P('grp'), may hold values from 0 to 5, as said below
- layer_input: bfloat16 [8, 512, 1024], P('grp', 'ctx'), may hold values from -6 to 6
Outputs:
- grad_queries: bfloat16 [8, 512, 1024], P('grp', 'ctx')
- grad_keys: bfloat16 [8, 512, 128], P('grp', 'ctx')
- grad_values: bfloat16 [8, 512, 128], P('grp', 'ctx')
- grad_weight: float32 [1024, 1024], P('grp')
The draws below stay inside these ranges and needn't reach their ends.
Inputs may be any that keep to these rules, and one draw needn't show every extreme that they name: `segment_ids`: in each pack the ids never fall and number the 6 documents in order; every document has a token and one has exactly 384. `lse`: for a query at offset t of its document, log(t + 1) plus a value between 1 and 2.
All inputs are finite; a program needn't handle non-finite values.
Results may differ from the reference program's by a relative error of at most 0.014.
Values may be sent and summed in bfloat16 or wider, within the bound.
A program may use at most 64 MiB of HBM per device.

```python
import jax
import jax.numpy as jnp
from jax import lax

D = 1024
HD = 128
HQ = 8
TOK_DEV = 128
DOCS = 6
PACK = 512
PACKS = 8
MOST = 384
N_CTX = 4


def doc_plan(key):
    rest = PACK - MOST

    def one(pack):
        pack_key = jax.random.fold_in(key, pack)
        cuts = jax.random.permutation(jax.random.fold_in(pack_key, 11), rest - 1)[:DOCS - 2] + 1
        cuts = jnp.sort(cuts.astype(jnp.int32))
        edges = jnp.concatenate([jnp.zeros((1,), jnp.int32), cuts, jnp.full((1,), rest, jnp.int32)])
        pieces = edges[1:] - edges[:-1]
        place = jax.random.randint(jax.random.fold_in(pack_key, 12), (), 0, DOCS)
        slots = jnp.arange(DOCS, dtype=jnp.int32)
        before = pieces[jnp.minimum(slots, DOCS - 2)]
        after = pieces[jnp.maximum(slots - 1, 0)]
        lengths = jnp.where(slots == place, MOST, jnp.where(slots < place, before, after)).astype(jnp.int32)
        ends = jnp.cumsum(lengths).astype(jnp.int32)
        positions = jnp.arange(PACK, dtype=jnp.int32)
        closed = (ends[None, :] <= positions[:, None]).astype(jnp.int32)
        segment = jnp.sum(closed, axis=1).astype(jnp.int32)
        start = jnp.sum(closed * lengths[None, :], axis=1).astype(jnp.int32)
        return (segment, positions - start + 1)
    return jax.vmap(one)(jnp.arange(PACKS, dtype=jnp.int32))


def draw_segment_ids(key, part):
    segment, visible = doc_plan(key)
    return segment


def draw_lse(key, part):
    segment, visible = doc_plan(key)
    offset = jax.random.uniform(jax.random.fold_in(key, 13), (PACKS, HQ, PACK), jnp.float32, 1.0, 2.0)
    return jnp.log(visible.astype(jnp.float32))[:, None, :] + offset


def with_spikes(values, rng, source, target, parts, factor):
    def block_of(dim):
        return (jnp.arange(values.shape[dim]) // (values.shape[dim] // parts)).reshape((-1,) + (1,) * (values.ndim - 1 - dim))

    one_side = jax.random.permutation(rng, parts)[block_of(target)]
    other_side = (block_of(target) + parts // 2) % parts
    return jnp.where((block_of(source) == one_side) | (block_of(source) == other_side), factor * values, values)


def levels(key, extent, shards, smallest, largest):
    gain, own = 1.0, jax.random.fold_in(key, 6)
    for dim, blocks in shards:
        heights = jnp.exp(jax.random.uniform(jax.random.fold_in(own, dim), (blocks,), jnp.float32, smallest / len(shards), largest / len(shards)))
        gain = gain * jnp.repeat(heights, extent[dim] // blocks).reshape([-1 if axis == dim else 1 for axis in range(len(extent))])
    return gain


def centred(key, extent, deviation, bound, split=(), held_as=jnp.bfloat16):
    gain = levels(key, extent, split, -0.22, 0.18) if split else 1.0
    entries = jax.random.normal(key, extent, jnp.float32) * deviation * gain
    return jnp.minimum(jnp.maximum(entries, -bound), bound).astype(held_as)


def bell_draw_with(stream_key, extent, spread, most, shards, heavy, kind=jnp.bfloat16):
    array = spread * jax.random.normal(stream_key, extent, jnp.float32)
    if shards:
        array = array * levels(stream_key, extent, shards, -0.22, 0.18)
    return jnp.clip(with_spikes(array, jax.random.fold_in(stream_key, 3), *heavy), -most, most).astype(kind)


def setup_inputs(seed: int = 0) -> dict:
    key_list = jax.random.split(jax.random.key(seed), 9)
    queries = jnp.clip(jax.random.uniform(key_list[0], (PACKS, PACK, HQ * HD), jnp.float32, -3.0, 3.0) * levels(key_list[0], (PACKS, PACK, HQ * HD), ((0, 8), (1, 4)), -0.4, 0.0), -3.0, 3.0).astype(jnp.bfloat16)
    keys = jnp.clip(jax.random.uniform(key_list[1], (PACKS, PACK, HD), jnp.float32, -1.6953125, 1.6953125) * levels(key_list[1], (PACKS, PACK, HD), ((0, 8), (1, 4)), -0.4, 0.0), -1.6953125, 1.6953125).astype(jnp.bfloat16)
    values = jnp.clip(jax.random.uniform(key_list[2], (PACKS, PACK, HD), jnp.float32, -1.6953125, 1.6953125) * levels(key_list[2], (PACKS, PACK, HD), ((0, 8), (1, 4)), -0.4, 0.0), -1.6953125, 1.6953125).astype(jnp.bfloat16)
    d_out = centred(key_list[3], (PACKS, PACK, HQ * HD), 1.0, 6.0, ((0, 8), (1, 4)))
    fwd_out = centred(key_list[4], (PACKS, PACK, HQ * HD), 0.1, 0.59765625, ((0, 8), (1, 4)))
    lse = draw_lse(jax.random.fold_in(key_list[8], 71), 0)
    segment_ids = draw_segment_ids(jax.random.fold_in(key_list[8], 71), 0)
    layer_input = bell_draw_with(key_list[7], (PACKS, PACK, D), 1.0, 6.0, ((0, 8), (1, 4)), (0, 2, 8, 2.0))
    return dict(queries=queries, keys=keys, values=values, d_out=d_out, fwd_out=fwd_out, lse=lse, segment_ids=segment_ids, layer_input=layer_input)


def pack_grads(queries, keys, values, d_out, fwd_out, lse, segment_ids):
    scale = HD ** -0.5
    q_heads = queries.reshape(PACK, HQ, HD)
    grad_heads = d_out.reshape(PACK, HQ, HD)
    delta = jnp.sum(grad_heads.astype(jnp.float32) * fwd_out.reshape(PACK, HQ, HD).astype(jnp.float32), axis=2)
    positions = jnp.arange(PACK, dtype=jnp.int32)
    keys_f = keys.astype(jnp.float32)
    values_f = values.astype(jnp.float32)

    def shard_grads(index):
        q_start = (index * TOK_DEV).astype(jnp.int32)
        q_part = lax.dynamic_slice_in_dim(q_heads, q_start, TOK_DEV, 0).astype(jnp.float32)
        g_part = lax.dynamic_slice_in_dim(grad_heads, q_start, TOK_DEV, 0).astype(jnp.float32)
        d_part = lax.dynamic_slice_in_dim(delta, q_start, TOK_DEV, 0)
        l_part = lax.dynamic_slice_in_dim(lse, q_start, TOK_DEV, 1)
        q_seg = lax.dynamic_slice_in_dim(segment_ids, q_start, TOK_DEV, 0)
        q_pos = lax.dynamic_slice_in_dim(positions, q_start, TOK_DEV, 0)
        visible = (q_seg[:, None] == segment_ids[None, :]) & (positions[None, :] <= q_pos[:, None])
        scores = jnp.einsum('qhd,kd->hqk', q_part, keys_f) * scale
        probs = jnp.where(visible[None], jnp.exp(scores - l_part[:, :, None]), 0.0)
        probs_b = lax.optimization_barrier(probs.astype(jnp.bfloat16)).astype(jnp.float32)
        dprobs = jnp.einsum('qhd,kd->hqk', g_part, values_f)
        dscores = probs * (dprobs - jnp.transpose(d_part)[:, :, None])
        ds_b = lax.optimization_barrier(dscores.astype(jnp.bfloat16)).astype(jnp.float32)
        grad_q = jnp.einsum('hqk,kd->qhd', ds_b, keys_f) * scale
        grad_k = jnp.einsum('hqk,qhd->kd', ds_b, q_part) * scale
        grad_v = jnp.einsum('hqk,qhd->kd', probs_b, g_part)
        joined = jnp.concatenate([grad_k, grad_v], axis=1).astype(jnp.bfloat16)
        return grad_q.reshape(TOK_DEV, HQ * HD), joined

    grad_q, joined = lax.map(shard_grads, jnp.arange(N_CTX, dtype=jnp.int32))
    grad_q = grad_q.reshape(PACK, HQ * HD).astype(jnp.bfloat16)
    summed = jnp.sum(joined.astype(jnp.float32), axis=0)
    return grad_q, summed[:, :HD].astype(jnp.bfloat16), summed[:, HD:].astype(jnp.bfloat16)


def reference(queries, keys, values, d_out, fwd_out, lse, segment_ids, layer_input):
    def one_pack(pack):
        return pack_grads(queries[pack], keys[pack], values[pack], d_out[pack], fwd_out[pack], lse[pack], segment_ids[pack])

    grad_queries, grad_keys, grad_values = lax.map(one_pack, jnp.arange(PACKS, dtype=jnp.int32))
    flat_input = layer_input.reshape(PACKS * PACK, D)
    flat_grad = grad_queries.reshape(PACKS * PACK, HQ * HD)
    grad_weight = lax.dot_general(flat_input, flat_grad, (((0,), (0,)), ((), ())), preferred_element_type=jnp.float32)
    return grad_queries, grad_keys, grad_values, grad_weight
```

```python
import functools

import jax
import jax.numpy as jnp
from jax import lax
from jax.experimental import pallas as pl
from jax.experimental.pallas import tpu as pltpu
from jax.sharding import PartitionSpec as P

MESH = pl.DeviceIdType.MESH
LANES = 128
PER_CHUNK = 2
AHEAD = (2, 3, 3, 5)
NT = (((1,), (1,)), ((), ()))
TN = (((0,), (0,)), ((), ()))


def dot(a, b, dims=(((1,), (0,)), ((), ()))):
    return lax.dot_general(a, b, dims, preferred_element_type=jnp.float32)


def kernel(n, grp, heads, hp, q_hbm, k_ref, v_ref, g_hbm, f_hbm, lse_hbm, seg_hbm, x_ref,
           dq_ref, dk_ref, dv_ref, gw_ref,
           lse_ref, seg_ref, q_ref, g_ref, f_ref, kbuf, vbuf, xbuf, in_sem, mask, delta, dk_acc, dv_acc, dq_acc, dqbuf, dw, e_send, e_recv,
           u_send, u_recv, d_send, d_recv, kv_send, kv_recv,
           k_ss, v_ss, k_rs, v_rs, x_ss, x_rs, q_ss, q_rs, e_ss, e_rs,
           u_ss, u_rs, d_ss, d_rs, p_ss, p_rs):
    c = lax.axis_index("ctx")
    g = lax.axis_index("grp")
    chips = grp // 2
    chip, core = g // 2, lax.rem(g, 2)
    tok, hd = k_ref.shape[1], k_ref.shape[2]
    scale = hd ** (-0.5)
    chunks = heads // hp
    cw = hp * hd
    rows = gw_ref.shape[0]

    xn = chip + 1 - 2 * lax.rem(chip, 2)
    yn = lax.rem(chip + 2, chips)
    diag = lax.rem(xn + 2, chips)
    others = (xn, yn, diag)
    half = tok // 2

    own_x = x_ref.at[0, :, pl.ds(pl.multiple_of(chip * 2 * rows, LANES), 2 * rows)]
    loads = [
        pltpu.make_async_copy(src, dst, in_sem.at[i])
        for i, (src, dst) in enumerate((
            (g_hbm, g_ref), (f_hbm, f_ref), (k_ref.at[0], kbuf.at[c]), (v_ref.at[0], vbuf.at[c]),
            (q_hbm, q_ref), (own_x, xbuf.at[chip]), (lse_hbm, lse_ref), (seg_hbm, seg_ref)))
    ]
    for load in loads:
        load.start()

    barrier = pltpu.get_barrier_semaphore()
    for t in range(1, n):
        pl.semaphore_signal(barrier, inc=1, device_id={"ctx": lax.rem(c + t, n)}, device_id_type=MESH)
    for other in others:
        pl.semaphore_signal(barrier, inc=1, device_id={"grp": other * 2 + core}, device_id_type=MESH)
    pl.semaphore_signal(barrier, inc=1, device_id={"grp": chip * 2 + 1 - core}, device_id_type=MESH)
    pl.semaphore_wait(barrier, n - 1 + chips)

    def key_copy(t):
        to = lax.rem(c + t, n)
        return [
            pltpu.make_async_remote_copy(
                src_ref=src.at[0], dst_ref=buf.at[c], send_sem=ss.at[t - 1], recv_sem=rs.at[c],
                device_id={"ctx": to}, device_id_type=MESH)
            for src, buf, ss, rs in ((k_ref, kbuf, k_ss, k_rs), (v_ref, vbuf, v_ss, v_rs))
        ]

    def key_arrival(j):
        return [
            pltpu.make_async_remote_copy(
                src_ref=src.at[0], dst_ref=buf.at[j], send_sem=ss.at[0], recv_sem=rs.at[j],
                device_id={"ctx": lax.rem(c + 1, n)}, device_id_type=MESH)
            for src, buf, ss, rs in ((k_ref, kbuf, k_ss, k_rs), (v_ref, vbuf, v_ss, v_rs))
        ]

    def x_copy(t):
        to = others[t]
        return pltpu.make_async_remote_copy(
            src_ref=x_ref.at[0, :, pl.ds(pl.multiple_of(to * 2 * rows, LANES), 2 * rows)],
            dst_ref=xbuf.at[chip], send_sem=x_ss.at[t], recv_sem=x_rs.at[t],
            device_id={"grp": to * 2 + core}, device_id_type=MESH)

    def q_copy(p, way):
        slot, part, to = (
            (chip, pl.ds(0, tok), xn), (chip, pl.ds(0, tok), yn),
            (xn, pl.ds(0, half), yn), (yn, pl.ds(half, half), xn))[way]
        return pltpu.make_async_remote_copy(
            src_ref=dqbuf.at[p, slot, part], dst_ref=dqbuf.at[p, slot, part],
            send_sem=q_ss.at[p, way], recv_sem=q_rs.at[p, way],
            device_id={"grp": to * 2 + core}, device_id_type=MESH)

    def pair_copy(p):
        return pltpu.make_async_remote_copy(
            src_ref=e_send.at[p], dst_ref=e_recv.at[p], send_sem=e_ss.at[p], recv_sem=e_rs.at[p],
            device_id={"grp": chip * 2 + 1 - core}, device_id_type=MESH)

    def up_copy(p):
        return pltpu.make_async_remote_copy(
            src_ref=u_send.at[p], dst_ref=u_recv.at[p], send_sem=u_ss.at[p], recv_sem=u_rs.at[p],
            device_id={"ctx": lax.rem(c + 1, n)}, device_id_type=MESH)

    def down_copy(p):
        return pltpu.make_async_remote_copy(
            src_ref=d_send.at[p], dst_ref=d_recv.at[p], send_sem=d_ss.at[p], recv_sem=d_rs.at[p],
            device_id={"ctx": lax.rem(c + n - 1, n)}, device_id_type=MESH)

    def part_copy(t):
        owner = lax.rem(c + n - t, n)
        return pltpu.make_async_remote_copy(
            src_ref=kv_send.at[owner], dst_ref=kv_recv.at[t - 1],
            send_sem=p_ss.at[t - 1], recv_sem=p_rs.at[t - 1],
            device_id={"ctx": owner}, device_id_type=MESH)

    for t in range(1, n):
        @pl.when(c + t < n)
        def _():
            for copy in key_copy(t):
                copy.start()
    for t in range(3):
        x_copy(t).start()

    for load in loads:
        load.wait()

    lane = lax.broadcasted_iota(jnp.int32, (tok, tok), 1)
    sub = lax.broadcasted_iota(jnp.int32, (tok, tok), 0)
    columns = jnp.zeros((tok, tok), jnp.float32)
    for h in range(heads):
        cols = slice(h * hd, (h + 1) * hd)
        total = jnp.sum(
            g_ref[0, :, cols].astype(jnp.float32) * f_ref[0, :, cols].astype(jnp.float32),
            axis=1, keepdims=True)
        columns = jnp.where(lane == h, total, columns)
    delta[...] = jnp.transpose(columns)[:heads]

    q_seg = seg_ref[:, pl.ds(pl.multiple_of(c * tok, LANES), tok)]

    def make_mask(j, _):
        k_seg = seg_ref[:, pl.ds(pl.multiple_of(j * tok, LANES), tok)]
        k_cols = jnp.transpose(jnp.broadcast_to(k_seg, (tok, tok)).astype(jnp.float32))
        same = k_cols == jnp.broadcast_to(q_seg, (tok, tok)).astype(jnp.float32)
        mask[j] = jnp.where(same & (j * tok + sub <= c * tok + lane), 1.0, 0.0)
        dk_acc[j] = jnp.zeros((tok, hd), jnp.float32)
        dv_acc[j] = jnp.zeros((tok, hd), jnp.float32)
        return 0

    lax.fori_loop(0, c + 1, make_mask, 0)

    def attend(p):
        parts = [p * hp + i for i in range(hp)]
        stack = lambda ref: jnp.concatenate([ref[0, :, h * hd:(h + 1) * hd] for h in parts], axis=0)
        dq_acc[...] = jnp.zeros_like(dq_acc)

        def tile(t, _):
            j = c - t
            if p == 0:
                @pl.when(t > 0)
                def _():
                    for copy in key_arrival(j):
                        copy.wait_recv()
            kj, vj = kbuf[j], vbuf[j]
            qs, gs = stack(q_ref), stack(g_ref)
            seen = jnp.concatenate([mask[j]] * hp, axis=1) > 0.0
            lse_row = jnp.concatenate([lse_ref[0, h:h + 1, :] for h in parts], axis=1)
            delta_row = jnp.concatenate([delta[h:h + 1, :] for h in parts], axis=1)
            probs = jnp.where(seen, jnp.exp(dot(kj, qs, NT) * scale - lse_row), 0.0)
            ds = (probs * (dot(vj, gs, NT) - delta_row)).astype(jnp.bfloat16)
            dv_acc[j] += dot(probs.astype(jnp.bfloat16), gs)
            dk_acc[j] += dot(ds, qs)
            dq_acc[...] += dot(ds, kj, TN)
            return 0

        lax.fori_loop(0, c + 1, tile, 0)
        dq = (dq_acc[...] * scale).astype(jnp.bfloat16)
        dq = jnp.concatenate([dq[i * tok:(i + 1) * tok] for i in range(hp)], axis=1)
        dq_ref[0, :, p * cw:(p + 1) * cw] = dq
        dqbuf[p, chip] = dq
        q_copy(p, 0).start()
        q_copy(p, 1).start()

    def send_parts():
        def pack(j, _):
            kv_send[j, 0] = (dk_acc[j] * scale).astype(jnp.bfloat16)
            kv_send[j, 1] = dv_acc[j].astype(jnp.bfloat16)
            return 0

        lax.fori_loop(0, c, pack, 0)
        for t in range(1, n):
            @pl.when(c >= t)
            def _():
                part_copy(t).start()

    def forward(p):
        for way in range(2):
            q_copy(p, way).wait_recv()
            q_copy(p, way + 2).start()

    def multiply(p):
        if p == 0:
            for t in range(3):
                x_copy(t).wait_recv()
        for way in (2, 3):
            q_copy(p, way).wait_recv()
        x = xbuf[...].reshape(chips * tok, 2 * rows)
        product = dot(x, dqbuf[p].reshape(chips * tok, cw), TN)
        dw[p] = product.reshape(2, rows, cw)
        e_send[p] = dw[p, 1 - core].astype(jnp.bfloat16)
        pair_copy(p).start()

    def exchange(p):
        pair_copy(p).wait_recv()
        own = dw[p, core] + e_recv[p].astype(jnp.float32)
        gw_ref[:, p * cw:(p + 1) * cw] = own
        dw[p, core] = own

        @pl.when(c == 0)
        def _():
            u_send[p] = own.astype(jnp.bfloat16)
            up_copy(p).start()

        @pl.when(c == n - 1)
        def _():
            d_send[p] = own.astype(jnp.bfloat16)
            down_copy(p).start()

    def running(p, first, last, copy, send, recv):
        cols = pl.ds(pl.multiple_of(p * cw, LANES), cw)

        @pl.when(jnp.logical_not(first))
        def _():
            copy(p).wait_recv()
            got = recv[p].astype(jnp.float32)

            @pl.when(jnp.logical_not(last))
            def _():
                send[p] = (got + dw[p, core]).astype(jnp.bfloat16)
                copy(p).start()
            gw_ref[:, cols] += got

    def hop(step):
        up, down = step - c, step - (n - 1 - c)

        @pl.when((up >= 0) & (up < chunks))
        def _():
            running(up, c == 0, c == n - 1, up_copy, u_send, u_recv)

        @pl.when((down >= 0) & (down < chunks))
        def _():
            running(down, c == n - 1, c == 0, down_copy, d_send, d_recv)

    at_forward, at_multiply, at_exchange, at_hop = AHEAD
    for step in range(at_hop + chunks + n - 1):
        if step < chunks:
            attend(step)
        if step == chunks - 1:
            send_parts()
        if 0 <= step - at_forward < chunks:
            forward(step - at_forward)
        if 0 <= step - at_multiply < chunks:
            multiply(step - at_multiply)
        if 0 <= step - at_exchange < chunks:
            exchange(step - at_exchange)
        if 1 <= step - at_hop:
            hop(step - at_hop)

    dk_acc[c] = dk_acc[c] * scale
    for t in range(1, n):
        @pl.when(c + t < n)
        def _():
            part_copy(t).wait_recv()
            dk_acc[c] += kv_recv[t - 1, 0].astype(jnp.float32)
            dv_acc[c] += kv_recv[t - 1, 1].astype(jnp.float32)
    dk_ref[0] = dk_acc[c].astype(jnp.bfloat16)
    dv_ref[0] = dv_acc[c].astype(jnp.bfloat16)

    for t in range(1, n):
        @pl.when(c + t < n)
        def _():
            for copy in key_copy(t):
                copy.wait_send()

        @pl.when(c >= t)
        def _():
            part_copy(t).wait_send()
    for t in range(3):
        x_copy(t).wait_send()
    for p in range(chunks):
        for way in range(4):
            q_copy(p, way).wait_send()
        pair_copy(p).wait_send()

        @pl.when(c < n - 1)
        def _():
            up_copy(p).wait_send()

        @pl.when(c > 0)
        def _():
            down_copy(p).wait_send()


def store(*refs):
    sources, targets, sem = refs[:4], refs[4:8], refs[8]
    copies = [pltpu.make_async_copy(a, b, sem.at[i]) for i, (a, b) in enumerate(zip(sources, targets))]
    for copy in copies:
        copy.start()
    for copy in copies:
        copy.wait()


def fused(n, grp, queries, keys, values, d_out, fwd_out, lse, segment_ids, layer_input):
    tok, hd, heads = keys.shape[1], keys.shape[2], lse.shape[1]
    width, rows = queries.shape[2], layer_input.shape[2] // grp
    chips, hp = grp // 2, PER_CHUNK
    chunks, cw = heads // hp, hp * hd
    bf, f32 = jnp.bfloat16, jnp.float32
    dma = pltpu.SemaphoreType.DMA
    vmem = pl.BlockSpec(memory_space=pltpu.VMEM)
    hbm = pl.BlockSpec(memory_space=pl.ANY)
    shapes = (
        jax.ShapeDtypeStruct((1, tok, width), bf),
        jax.ShapeDtypeStruct((1, tok, hd), bf),
        jax.ShapeDtypeStruct((1, tok, hd), bf),
        jax.ShapeDtypeStruct((rows, width), f32),
    )
    inputs = (queries, keys, values, d_out, fwd_out, lse, segment_ids, layer_input)
    results = pl.pallas_call(
        functools.partial(kernel, n, grp, heads, hp),
        out_shape=shapes,
        in_specs=[hbm] * 8,
        out_specs=(vmem,) * 4,
        scratch_shapes=[
            pltpu.VMEM((1, heads, tok), f32), pltpu.VMEM((1, tok * n), jnp.int32),
            pltpu.VMEM((1, tok, width), bf), pltpu.VMEM((1, tok, width), bf), pltpu.VMEM((1, tok, width), bf),
            pltpu.VMEM((n, tok, hd), bf), pltpu.VMEM((n, tok, hd), bf),
            pltpu.VMEM((chips, tok, 2 * rows), bf), dma((8,)),
            pltpu.VMEM((n, tok, tok), f32), pltpu.VMEM((heads, tok), f32),
            pltpu.VMEM((n, tok, hd), f32), pltpu.VMEM((n, tok, hd), f32),
            pltpu.VMEM((hp * tok, hd), f32),
            pltpu.VMEM((chunks, chips, tok, cw), bf),
            pltpu.VMEM((chunks, 2, rows, cw), f32),
            pltpu.VMEM((chunks, rows, cw), bf), pltpu.VMEM((chunks, rows, cw), bf),
            pltpu.VMEM((chunks, rows, cw), bf), pltpu.VMEM((chunks, rows, cw), bf),
            pltpu.VMEM((chunks, rows, cw), bf), pltpu.VMEM((chunks, rows, cw), bf),
            pltpu.VMEM((n, 2, tok, hd), bf), pltpu.VMEM((n - 1, 2, tok, hd), bf),
            dma((n - 1,)), dma((n - 1,)), dma((n,)), dma((n,)),
            dma((3,)), dma((3,)),
            dma((chunks, 4)), dma((chunks, 4)),
            dma((chunks,)), dma((chunks,)), dma((chunks,)), dma((chunks,)),
            dma((chunks,)), dma((chunks,)), dma((n - 1,)), dma((n - 1,)),
        ],
        compiler_params=pltpu.CompilerParams(collective_id=0, has_side_effects=True, vmem_limit_bytes=24 << 20),
    )(*[pltpu.with_memory_space_constraint(a, pltpu.HBM) for a in inputs])
    return pl.pallas_call(
        store,
        out_shape=shapes,
        in_specs=[vmem] * 4,
        out_specs=(hbm,) * 4,
        scratch_shapes=[dma((4,))],
        compiler_params=pltpu.CompilerParams(vmem_limit_bytes=8 << 20),
    )(*results)


def on_device(queries, keys, values, d_out, fwd_out, lse, segment_ids, layer_input):
    tok = queries.shape[1]
    heads = lse.shape[1]
    head_dim = keys.shape[2]
    scale = head_dim ** (-0.5)
    seg_all = segment_ids[0]
    q_start = lax.axis_index("ctx") * tok
    q_heads = queries[0].reshape(tok, heads, head_dim)
    grad_heads = d_out[0].reshape(tok, heads, head_dim)
    delta = jnp.sum(
        grad_heads.astype(jnp.float32)
        * fwd_out[0].reshape(tok, heads, head_dim).astype(jnp.float32),
        axis=2,
    )
    delta_rows = jnp.transpose(delta)
    lse_rows = lse[0]
    q_seg = lax.dynamic_slice_in_dim(seg_all, q_start, tok, 0)
    q_pos = q_start + jnp.arange(tok, dtype=jnp.int32)
    key_rows = lax.all_gather(keys, "ctx", axis=1, tiled=True)[0]
    value_rows = lax.all_gather(values, "ctx", axis=1, tiled=True)[0]
    count = key_rows.shape[0]
    k_pos = jnp.arange(count, dtype=jnp.int32)
    visible = (q_seg[:, None] == seg_all[None, :]) & (k_pos[None, :] <= q_pos[:, None])
    scores = (
        jnp.einsum("qhd,kd->hqk", q_heads, key_rows, preferred_element_type=jnp.float32) * scale
    )
    probs = jnp.where(visible[None], jnp.exp(scores - lse_rows[:, :, None]), 0.0)
    probs_b = probs.astype(jnp.bfloat16)
    dprobs = jnp.einsum("qhd,kd->hqk", grad_heads, value_rows, preferred_element_type=jnp.float32)
    dscores = (probs * (dprobs - delta_rows[:, :, None])).astype(jnp.bfloat16)
    dq_acc = (
        jnp.einsum("hqk,kd->qhd", dscores, key_rows, preferred_element_type=jnp.float32) * scale
    )
    grad_k = jnp.einsum("hqk,qhd->kd", dscores, q_heads, preferred_element_type=jnp.float32) * scale
    grad_v = jnp.einsum("hqk,qhd->kd", probs_b, grad_heads, preferred_element_type=jnp.float32)
    block = jnp.concatenate([grad_k, grad_v], axis=1)
    dkv_acc = block
    dq_acc, dkv_acc = (dq_acc, dkv_acc)
    grad_q = dq_acc.reshape(tok, heads * head_dim).astype(jnp.bfloat16)
    owned = lax.psum_scatter(
        dkv_acc.astype(jnp.bfloat16), "ctx", scatter_dimension=0, tiled=True
    ).astype(jnp.float32)
    grad_k = owned[:, :head_dim].astype(jnp.bfloat16)
    grad_v = owned[:, head_dim:].astype(jnp.bfloat16)
    inputs = layer_input[0]
    rows_part = lax.psum_scatter(
        lax.dot_general(
            inputs, grad_q, (((0,), (0,)), ((), ())), preferred_element_type=jnp.float32
        ),
        "grp",
        scatter_dimension=0,
        tiled=True,
    )
    grad_weight = lax.psum(rows_part.astype(jnp.bfloat16), "ctx").astype(jnp.float32)
    return (grad_q[None], grad_k[None], grad_v[None], grad_weight)


def solution(mesh):
    n, grp = mesh.shape["ctx"], mesh.shape["grp"]

    def either(*args):
        tok, depth = args[7].shape[1], args[7].shape[2]
        heads, hd = args[5].shape[1], args[1].shape[2]
        gather = grp == 8 and n > 1 and grp * tok <= depth
        tiled = (depth // grp) % LANES == 0 and tok % LANES == 0 and hd == tok and heads % PER_CHUNK == 0
        return fused(n, grp, *args) if gather and tiled and heads <= tok else on_device(*args)

    return jax.shard_map(
        either,
        mesh=mesh,
        in_specs=(
            P("grp", "ctx", None),
            P("grp", "ctx", None),
            P("grp", "ctx", None),
            P("grp", "ctx", None),
            P("grp", "ctx", None),
            P("grp", None, "ctx"),
            P("grp", None),
            P("grp", "ctx", None),
        ),
        out_specs=(
            P("grp", "ctx", None),
            P("grp", "ctx", None),
            P("grp", "ctx", None),
            P("grp", None),
        ),
        check_vma=False,
    )
```

```python
import functools

import jax
import jax.numpy as jnp
from jax import lax
from jax.experimental import pallas as pl
from jax.experimental.pallas import tpu as pltpu
from jax.sharding import PartitionSpec as P

MESH = pl.DeviceIdType.MESH
LANES = 128
HIDDEN = -1e30
AHEAD = 2
NT = (((1,), (1,)), ((), ()))
TN = (((0,), (0,)), ((), ()))


def dot(a, b, dims=(((1,), (0,)), ((), ()))):
    return lax.dot_general(a, b, dims, preferred_element_type=jnp.float32)


def kernel(n, grp, heads, q_hbm, k_hbm, v_hbm, g_hbm, f_hbm, lse_hbm, seg_hbm, x_hbm,
           dq_ref, dk_ref, dv_ref, gw_ref,
           lse_ref, seg_ref, q_ref, g_ref, f_ref, kbuf, vbuf, xbuf, in_sem,
           bias, delta, kt, xt, dk_acc, dv_acc, dqt_acc, dqbuf, own, e_send, e_recv,
           r_send, r_recv, f_send, f_recv, a_send, a_recv, kv_send, kv_recv,
           k_ss, v_ss, k_rs, v_rs, x_ss, x_rs, q_ss, q_rs, e_ss, e_rs,
           r_ss, r_rs, f_ss, f_rs, a_ss, a_rs, p_ss, p_rs):
    c = lax.axis_index("ctx")
    g = lax.axis_index("grp")
    chips = grp // 2
    chip, core = g // 2, lax.rem(g, 2)
    tok, hd = k_hbm.shape[1], k_hbm.shape[2]
    scale = hd ** (-0.5)
    hp = heads // n
    cw = hp * hd
    rows = gw_ref.shape[0]
    bf, f32 = jnp.bfloat16, jnp.float32

    xn = chip + 1 - 2 * lax.rem(chip, 2)
    yn = lax.rem(chip + 2, chips)
    others = (xn, yn, lax.rem(xn + 2, chips))

    own_x = x_hbm.at[0, :, pl.ds(pl.multiple_of(chip * 2 * rows, LANES), 2 * rows)]
    loads = [
        pltpu.make_async_copy(src, dst, in_sem.at[i])
        for i, (src, dst) in enumerate((
            (seg_hbm, seg_ref), (lse_hbm, lse_ref), (g_hbm, g_ref), (f_hbm, f_ref),
            (k_hbm.at[0], kbuf.at[c]), (v_hbm.at[0], vbuf.at[c]), (q_hbm, q_ref), (own_x, xbuf.at[chip])))
    ]
    for load in loads:
        load.start()

    barrier = pltpu.get_barrier_semaphore()
    for t in range(1, n):
        pl.semaphore_signal(barrier, inc=1, device_id={"ctx": lax.rem(c + t, n)}, device_id_type=MESH)
    for other in others:
        pl.semaphore_signal(barrier, inc=1, device_id={"grp": other * 2 + core}, device_id_type=MESH)
    pl.semaphore_signal(barrier, inc=1, device_id={"grp": chip * 2 + 1 - core}, device_id_type=MESH)

    def key_copy(t):
        return [
            pltpu.make_async_remote_copy(
                src_ref=src.at[0], dst_ref=buf.at[c], send_sem=ss.at[t - 1], recv_sem=rs.at[c],
                device_id={"ctx": lax.rem(c + t, n)}, device_id_type=MESH)
            for src, buf, ss, rs in ((k_hbm, kbuf, k_ss, k_rs), (v_hbm, vbuf, v_ss, v_rs))
        ]

    def key_arrival(j):
        return [
            pltpu.make_async_remote_copy(
                src_ref=src.at[0], dst_ref=buf.at[j], send_sem=ss.at[0], recv_sem=rs.at[j],
                device_id={"ctx": lax.rem(c + 1, n)}, device_id_type=MESH)
            for src, buf, ss, rs in ((k_hbm, kbuf, k_ss, k_rs), (v_hbm, vbuf, v_ss, v_rs))
        ]

    def x_copy(t):
        return pltpu.make_async_remote_copy(
            src_ref=x_hbm.at[0, :, pl.ds(pl.multiple_of(others[t] * 2 * rows, LANES), 2 * rows)],
            dst_ref=xbuf.at[chip], send_sem=x_ss.at[t], recv_sem=x_rs.at[t],
            device_id={"grp": others[t] * 2 + core}, device_id_type=MESH)

    half = cw // 2

    def q_copy(p, way):
        slot, part, to = (
            (chip, pl.ds(0, cw), xn), (chip, pl.ds(0, cw), yn),
            (xn, pl.ds(0, half), yn), (yn, pl.ds(half, half), xn))[way]
        return pltpu.make_async_remote_copy(
            src_ref=dqbuf.at[p, slot, part], dst_ref=dqbuf.at[p, slot, part],
            send_sem=q_ss.at[p, way], recv_sem=q_rs.at[p, way],
            device_id={"grp": to * 2 + core}, device_id_type=MESH)

    def pair_copy(p):
        return pltpu.make_async_remote_copy(
            src_ref=e_send.at[p], dst_ref=e_recv.at[p], send_sem=e_ss.at[p], recv_sem=e_rs.at[p],
            device_id={"grp": chip * 2 + 1 - core}, device_id_type=MESH)

    side = lax.rem(c, 2)
    near, far = c + 1 - 2 * side, lax.rem(c + 2, n)
    hw = cw // 2

    def near_copy(p):
        return pltpu.make_async_remote_copy(
            src_ref=r_send.at[p], dst_ref=r_recv.at[p], send_sem=r_ss.at[p], recv_sem=r_rs.at[p],
            device_id={"ctx": near}, device_id_type=MESH)

    def far_copy(p):
        return pltpu.make_async_remote_copy(
            src_ref=f_send.at[p], dst_ref=f_recv.at[p], send_sem=f_ss.at[p], recv_sem=f_rs.at[p],
            device_id={"ctx": far}, device_id_type=MESH)

    def sum_copy(p):
        return pltpu.make_async_remote_copy(
            src_ref=a_send.at[p], dst_ref=a_recv.at[p], send_sem=a_ss.at[p], recv_sem=a_rs.at[p],
            device_id={"ctx": near}, device_id_type=MESH)

    def part_copy(t):
        owner = lax.rem(c + n - t, n)
        return pltpu.make_async_remote_copy(
            src_ref=kv_send.at[owner], dst_ref=kv_recv.at[t - 1],
            send_sem=p_ss.at[t - 1], recv_sem=p_rs.at[t - 1],
            device_id={"ctx": owner}, device_id_type=MESH)

    pl.semaphore_wait(barrier, n - 1 + chips)
    for t in range(n - 1, 0, -1):
        @pl.when(c + t < n)
        def _():
            for copy in key_copy(t):
                copy.start()
    for t in range(3):
        x_copy(t).start()

    loads[0].wait()
    lane = lax.broadcasted_iota(jnp.int32, (tok, tok), 1)
    sub = lax.broadcasted_iota(jnp.int32, (tok, tok), 0)
    q_seg = seg_ref[:, pl.ds(pl.multiple_of(c * tok, LANES), tok)]

    def make_bias(j, _):
        k_seg = seg_ref[:, pl.ds(pl.multiple_of(j * tok, LANES), tok)]
        k_cols = jnp.transpose(jnp.broadcast_to(k_seg, (tok, tok)).astype(f32))
        same = k_cols == jnp.broadcast_to(q_seg, (tok, tok)).astype(f32)
        bias[j] = jnp.where(same & (j * tok + sub <= c * tok + lane), 0.0, HIDDEN)
        return 0

    lax.fori_loop(0, c + 1, make_bias, 0)

    for load in loads[1:4]:
        load.wait()
    head = lax.broadcasted_iota(jnp.int32, (heads, heads * hd), 0)
    column = lax.broadcasted_iota(jnp.int32, (heads, heads * hd), 1)
    pick = jnp.where(column // hd == head, 1.0, 0.0).astype(bf)
    terms = g_ref[0].astype(f32) * f_ref[0].astype(f32)
    high = terms.astype(bf)
    low = (terms - high.astype(f32)).astype(bf)
    delta[...] = dot(pick, high, NT) + dot(pick, low, NT)

    for load in loads[4:7]:
        load.wait()

    def stack(ref, p):
        return jnp.concatenate(
            [ref[0, :, pl.ds(pl.multiple_of(p * cw + i * hd, LANES), hd)] for i in range(hp)], axis=0)

    def row(load, p):
        return jnp.concatenate([load(p * hp + i) for i in range(hp)], axis=1)

    def tiles(p, k, v, hide):
        qs, gs = stack(q_ref, p), stack(g_ref, p)
        lse_row = row(lambda h: lse_ref[0, pl.ds(h, 1), :], p)
        delta_row = row(lambda h: delta[pl.ds(h, 1), :], p)
        hide = jnp.concatenate([hide] * hp, axis=1)
        probs = jnp.exp(dot(k, qs, NT) * scale - lse_row + hide)
        ds = (probs * (dot(v, gs, NT) - delta_row)).astype(bf)
        return ds, dot(probs.astype(bf), gs), dot(ds, qs)

    def finish(p, dqt):
        dqt = (dqt * scale).astype(bf)
        for i in range(hp):
            dqbuf[p, chip, i * hd:(i + 1) * hd] = dqt[:, i * tok:(i + 1) * tok]

        @pl.when(p > n - 1 - AHEAD)
        def _():
            q_copy(p, 0).start()
            q_copy(p, 1).start()

    def turn(block):
        return jnp.transpose(block.astype(f32)).astype(bf)

    kt[c] = turn(kbuf[c])
    dk_acc[c] = jnp.zeros((tok, hd), f32)
    dv_acc[c] = jnp.zeros((tok, hd), f32)

    def diagonal(i, last):
        p = n - 1 - i
        ds, dv, dk = tiles(p, kbuf[c], vbuf[c], bias[c])
        dv_acc[c] += dv
        dk_acc[c] += dk
        dqt = dot(kt[c], ds)
        if last:
            finish(p, dqt)
        else:
            dqt_acc[p] = dqt
        return 0

    def earlier(count):
        for j in range(count - 1, -1, -1):
            for copy in key_arrival(j):
                copy.wait_recv()
            kt[j] = turn(kbuf[j])
            dk_acc[j] = jnp.zeros((tok, hd), f32)
            dv_acc[j] = jnp.zeros((tok, hd), f32)

        def chunk(i, _):
            p = n - 1 - i
            ds, dv, dk = tiles(
                p, kbuf[:count].reshape(count * tok, hd), vbuf[:count].reshape(count * tok, hd),
                bias[:count].reshape(count * tok, tok))
            dqt = dqt_acc[p] + dot(jnp.concatenate([kt[j] for j in range(count)], axis=1), ds)
            finish(p, dqt)
            dv_acc[:count] += dv.reshape(count, tok, hd)
            dk_acc[:count] += dk.reshape(count, tok, hd)
            return 0

        lax.fori_loop(0, n, chunk, 0)
        for j in range(count):
            kv_send[j, 0] = (dk_acc[j] * scale).astype(bf)
            kv_send[j, 1] = dv_acc[j].astype(bf)
        for t in range(1, count + 1):
            part_copy(t).start()

    @pl.when(c == 0)
    def _():
        lax.fori_loop(0, n, lambda i, _: diagonal(i, True), 0)

    @pl.when(c > 0)
    def _():
        lax.fori_loop(0, n, lambda i, _: diagonal(i, False), 0)

    for count in range(1, n):
        @pl.when(c == count)
        def _():
            earlier(count)

    loads[7].wait()
    for t in range(3):
        x_copy(t).wait_recv()
    for s in range(chips):
        for i in range(2):
            which = lax.rem(core + i, 2)
            xt[i * rows:(i + 1) * rows, s * tok:(s + 1) * tok] = turn(
                xbuf[s, :, pl.ds(pl.multiple_of(which * rows, LANES), rows)])

    def gather_parts():
        dk_acc[c] = dk_acc[c] * scale
        for t in range(1, n):
            @pl.when(c + t < n)
            def _():
                part_copy(t).wait_recv()
                dk_acc[c] += kv_recv[t - 1, 0].astype(f32)
                dv_acc[c] += kv_recv[t - 1, 1].astype(f32)
        dk_ref[0] = dk_acc[c].astype(bf)
        dv_ref[0] = dv_acc[c].astype(bf)

    def forward(p):
        for way in range(2):
            q_copy(p, way).wait_recv()
            q_copy(p, way + 2).start()
        if p >= AHEAD:
            q_copy(p - AHEAD, 0).start()
            q_copy(p - AHEAD, 1).start()

    def multiply(p):
        for way in (2, 3):
            q_copy(p, way).wait_recv()
        product = dot(xt[...], jnp.concatenate([dqbuf[p, s] for s in range(chips)], axis=1), NT)
        e_send[p] = product[rows:].astype(bf)
        pair_copy(p).start()
        own[p] = product[:rows]
        for i in range(hp):
            dq_ref[0, :, p * cw + i * hd:p * cw + (i + 1) * hd] = turn(dqbuf[p, chip, i * hd:(i + 1) * hd])
        pair_copy(p).wait_recv()
        own[p] += e_recv[p].astype(f32)
        r_send[p] = own[p, :, pl.ds(pl.multiple_of((1 - side) * hw, LANES), hw)].astype(bf)
        near_copy(p).start()

    def across(p):
        near_copy(p).wait_recv()
        total = own[p, :, pl.ds(pl.multiple_of(side * hw, LANES), hw)] + r_recv[p].astype(f32)
        f_send[p] = total.astype(bf)
        far_copy(p).start()

    def settle(p):
        far_copy(p).wait_recv()
        a_send[p] = (f_send[p].astype(f32) + f_recv[p].astype(f32)).astype(bf)
        sum_copy(p).start()
        gw_ref[:, pl.ds(pl.multiple_of(p * cw + side * hw, LANES), hw)] = a_send[p].astype(f32)

    def collect(p):
        sum_copy(p).wait_recv()
        gw_ref[:, pl.ds(pl.multiple_of(p * cw + (1 - side) * hw, LANES), hw)] = a_recv[p].astype(f32)

    stages = (forward, multiply, across, settle, collect)
    for step in range(n + len(stages) - 1):
        if step == n:
            gather_parts()
        for stage, work in enumerate(stages):
            if 0 <= step - stage < n:
                work(n - 1 - (step - stage))

    for t in range(1, n):
        @pl.when(c + t < n)
        def _():
            for copy in key_copy(t):
                copy.wait_send()

        @pl.when(c >= t)
        def _():
            part_copy(t).wait_send()
    for t in range(3):
        x_copy(t).wait_send()
    for p in range(n):
        for way in range(4):
            q_copy(p, way).wait_send()
        for copy in (pair_copy(p), near_copy(p), far_copy(p), sum_copy(p)):
            copy.wait_send()


def store(*refs):
    sources, targets, sem = refs[:4], refs[4:8], refs[8]
    copies = [pltpu.make_async_copy(a, b, sem.at[i]) for i, (a, b) in enumerate(zip(sources, targets))]
    for copy in copies:
        copy.start()
    for copy in copies:
        copy.wait()


def fused(n, grp, queries, keys, values, d_out, fwd_out, lse, segment_ids, layer_input):
    tok, hd, heads = keys.shape[1], keys.shape[2], lse.shape[1]
    width, rows = queries.shape[2], layer_input.shape[2] // grp
    chips, cw = grp // 2, width // n
    bf, f32 = jnp.bfloat16, jnp.float32
    dma = pltpu.SemaphoreType.DMA
    vmem = pl.BlockSpec(memory_space=pltpu.VMEM)
    hbm = pl.BlockSpec(memory_space=pl.ANY)
    shapes = (
        jax.ShapeDtypeStruct((1, tok, width), bf),
        jax.ShapeDtypeStruct((1, tok, hd), bf),
        jax.ShapeDtypeStruct((1, tok, hd), bf),
        jax.ShapeDtypeStruct((rows, width), f32),
    )
    inputs = (queries, keys, values, d_out, fwd_out, lse, segment_ids, layer_input)
    results = pl.pallas_call(
        functools.partial(kernel, n, grp, heads),
        out_shape=shapes,
        in_specs=[hbm] * 8,
        out_specs=(vmem,) * 4,
        scratch_shapes=[
            pltpu.VMEM((1, heads, tok), f32), pltpu.VMEM((1, tok * n), jnp.int32),
            pltpu.VMEM((1, tok, width), bf), pltpu.VMEM((1, tok, width), bf), pltpu.VMEM((1, tok, width), bf),
            pltpu.VMEM((n, tok, hd), bf), pltpu.VMEM((n, tok, hd), bf),
            pltpu.VMEM((chips, tok, 2 * rows), bf), dma((8,)),
            pltpu.VMEM((n, tok, tok), f32), pltpu.VMEM((heads, tok), f32),
            pltpu.VMEM((n, hd, tok), bf), pltpu.VMEM((2 * rows, chips * tok), bf),
            pltpu.VMEM((n, tok, hd), f32), pltpu.VMEM((n, tok, hd), f32),
            pltpu.VMEM((n, hd, cw), f32), pltpu.VMEM((n, chips, cw, tok), bf),
            pltpu.VMEM((n, rows, cw), f32),
            pltpu.VMEM((n, rows, cw), bf), pltpu.VMEM((n, rows, cw), bf),
            *[pltpu.VMEM((n, rows, cw // 2), bf)] * 6,
            pltpu.VMEM((n, 2, tok, hd), bf), pltpu.VMEM((n - 1, 2, tok, hd), bf),
            dma((n - 1,)), dma((n - 1,)), dma((n,)), dma((n,)),
            dma((3,)), dma((3,)), dma((n, 4)), dma((n, 4)), dma((n,)), dma((n,)),
            *[dma((n,))] * 6, dma((n - 1,)), dma((n - 1,)),
        ],
        compiler_params=pltpu.CompilerParams(collective_id=0, has_side_effects=True, vmem_limit_bytes=24 << 20),
    )(*[pltpu.with_memory_space_constraint(a, pltpu.HBM) for a in inputs])
    return pl.pallas_call(
        store,
        out_shape=shapes,
        in_specs=[vmem] * 4,
        out_specs=(hbm,) * 4,
        scratch_shapes=[dma((4,))],
        compiler_params=pltpu.CompilerParams(vmem_limit_bytes=8 << 20),
    )(*results)


def on_device(queries, keys, values, d_out, fwd_out, lse, segment_ids, layer_input):
    tok = queries.shape[1]
    heads = lse.shape[1]
    head_dim = keys.shape[2]
    scale = head_dim ** (-0.5)
    seg_all = segment_ids[0]
    q_start = lax.axis_index("ctx") * tok
    q_heads = queries[0].reshape(tok, heads, head_dim)
    grad_heads = d_out[0].reshape(tok, heads, head_dim)
    delta = jnp.sum(
        grad_heads.astype(jnp.float32)
        * fwd_out[0].reshape(tok, heads, head_dim).astype(jnp.float32),
        axis=2,
    )
    delta_rows = jnp.transpose(delta)
    lse_rows = lse[0]
    q_seg = lax.dynamic_slice_in_dim(seg_all, q_start, tok, 0)
    q_pos = q_start + jnp.arange(tok, dtype=jnp.int32)
    key_rows = lax.all_gather(keys, "ctx", axis=1, tiled=True)[0]
    value_rows = lax.all_gather(values, "ctx", axis=1, tiled=True)[0]
    count = key_rows.shape[0]
    k_pos = jnp.arange(count, dtype=jnp.int32)
    visible = (q_seg[:, None] == seg_all[None, :]) & (k_pos[None, :] <= q_pos[:, None])
    scores = (
        jnp.einsum("qhd,kd->hqk", q_heads, key_rows, preferred_element_type=jnp.float32) * scale
    )
    probs = jnp.where(visible[None], jnp.exp(scores - lse_rows[:, :, None]), 0.0)
    probs_b = probs.astype(jnp.bfloat16)
    dprobs = jnp.einsum("qhd,kd->hqk", grad_heads, value_rows, preferred_element_type=jnp.float32)
    dscores = (probs * (dprobs - delta_rows[:, :, None])).astype(jnp.bfloat16)
    dq_acc = (
        jnp.einsum("hqk,kd->qhd", dscores, key_rows, preferred_element_type=jnp.float32) * scale
    )
    grad_k = jnp.einsum("hqk,qhd->kd", dscores, q_heads, preferred_element_type=jnp.float32) * scale
    grad_v = jnp.einsum("hqk,qhd->kd", probs_b, grad_heads, preferred_element_type=jnp.float32)
    block = jnp.concatenate([grad_k, grad_v], axis=1)
    dkv_acc = block
    dq_acc, dkv_acc = (dq_acc, dkv_acc)
    grad_q = dq_acc.reshape(tok, heads * head_dim).astype(jnp.bfloat16)
    owned = lax.psum_scatter(
        dkv_acc.astype(jnp.bfloat16), "ctx", scatter_dimension=0, tiled=True
    ).astype(jnp.float32)
    grad_k = owned[:, :head_dim].astype(jnp.bfloat16)
    grad_v = owned[:, head_dim:].astype(jnp.bfloat16)
    inputs = layer_input[0]
    rows_part = lax.psum_scatter(
        lax.dot_general(
            inputs, grad_q, (((0,), (0,)), ((), ())), preferred_element_type=jnp.float32
        ),
        "grp",
        scatter_dimension=0,
        tiled=True,
    )
    grad_weight = lax.psum(rows_part.astype(jnp.bfloat16), "ctx").astype(jnp.float32)
    return (grad_q[None], grad_k[None], grad_v[None], grad_weight)


def solution(mesh):
    n, grp = mesh.shape["ctx"], mesh.shape["grp"]

    def either(*args):
        tok, depth = args[7].shape[1], args[7].shape[2]
        heads, hd = args[5].shape[1], args[1].shape[2]
        gather = grp == 8 and n == 4 and grp * tok <= depth
        tiled = (depth // grp) % LANES == 0 and tok % LANES == 0 and hd == tok and heads % (2 * n) == 0
        return fused(n, grp, *args) if gather and tiled and heads <= tok else on_device(*args)

    return jax.shard_map(
        either,
        mesh=mesh,
        in_specs=(
            P("grp", "ctx", None),
            P("grp", "ctx", None),
            P("grp", "ctx", None),
            P("grp", "ctx", None),
            P("grp", "ctx", None),
            P("grp", None, "ctx"),
            P("grp", None),
            P("grp", "ctx", None),
        ),
        out_specs=(
            P("grp", "ctx", None),
            P("grp", "ctx", None),
            P("grp", "ctx", None),
            P("grp", None),
        ),
        check_vma=False,
    )
```

```python
import functools

import jax
import jax.numpy as jnp
from jax import lax
from jax.experimental import pallas as pl
from jax.experimental.pallas import tpu as pltpu
from jax.sharding import PartitionSpec as P

MESH = pl.DeviceIdType.MESH
LANES = 128
HIDDEN = -1e30
AHEAD = 3
NT = (((1,), (1,)), ((), ()))
TN = (((0,), (0,)), ((), ()))


def dot(a, b, dims=(((1,), (0,)), ((), ()))):
    return lax.dot_general(a, b, dims, preferred_element_type=jnp.float32)


def kernel(n, grp, heads, q_hbm, k_hbm, v_hbm, g_hbm, f_hbm, lse_hbm, seg_hbm, x_hbm,
           dq_ref, dk_ref, dv_ref, gw_ref,
           lse_ref, seg_ref, q_ref, g_ref, f_ref, kbuf, vbuf, xbuf, in_sem,
           bias, delta, kt, xt, dk_acc, dv_acc, dqt_acc, dqbuf, own, e_send, e_recv,
           r_send, r_recv, f_send, f_recv, a_send, a_recv, kv_send, kv_recv,
           k_ss, v_ss, k_rs, v_rs, x_ss, x_rs, q_ss, q_rs, e_ss, e_rs,
           r_ss, r_rs, f_ss, f_rs, a_ss, a_rs, p_ss, p_rs):
    c = lax.axis_index("ctx")
    g = lax.axis_index("grp")
    chips = grp // 2
    chip, core = g // 2, lax.rem(g, 2)
    tok, hd = k_hbm.shape[1], k_hbm.shape[2]
    scale = hd ** (-0.5)
    hp = heads // n
    cw = hp * hd
    rows = gw_ref.shape[0]
    bf, f32 = jnp.bfloat16, jnp.float32

    xn = chip + 1 - 2 * lax.rem(chip, 2)
    yn = lax.rem(chip + 2, chips)
    others = (xn, yn, lax.rem(xn + 2, chips))

    own_x = x_hbm.at[0, :, pl.ds(pl.multiple_of(chip * 2 * rows, LANES), 2 * rows)]
    loads = [
        pltpu.make_async_copy(src, dst, in_sem.at[i])
        for i, (src, dst) in enumerate((
            (seg_hbm, seg_ref), (lse_hbm, lse_ref), (g_hbm, g_ref), (f_hbm, f_ref),
            (k_hbm.at[0], kbuf.at[c]), (v_hbm.at[0], vbuf.at[c]), (q_hbm, q_ref), (own_x, xbuf.at[chip])))
    ]
    for load in loads:
        load.start()

    barrier = pltpu.get_barrier_semaphore()
    for t in range(1, n):
        pl.semaphore_signal(barrier, inc=1, device_id={"ctx": lax.rem(c + t, n)}, device_id_type=MESH)
    for other in others:
        pl.semaphore_signal(barrier, inc=1, device_id={"grp": other * 2 + core}, device_id_type=MESH)
    pl.semaphore_signal(barrier, inc=1, device_id={"grp": chip * 2 + 1 - core}, device_id_type=MESH)

    def key_copy(t):
        return [
            pltpu.make_async_remote_copy(
                src_ref=src.at[0], dst_ref=buf.at[c], send_sem=ss.at[t - 1], recv_sem=rs.at[c],
                device_id={"ctx": lax.rem(c + t, n)}, device_id_type=MESH)
            for src, buf, ss, rs in ((k_hbm, kbuf, k_ss, k_rs), (v_hbm, vbuf, v_ss, v_rs))
        ]

    def key_arrival(j):
        return [
            pltpu.make_async_remote_copy(
                src_ref=src.at[0], dst_ref=buf.at[j], send_sem=ss.at[0], recv_sem=rs.at[j],
                device_id={"ctx": lax.rem(c + 1, n)}, device_id_type=MESH)
            for src, buf, ss, rs in ((k_hbm, kbuf, k_ss, k_rs), (v_hbm, vbuf, v_ss, v_rs))
        ]

    def x_copy(t):
        return pltpu.make_async_remote_copy(
            src_ref=x_hbm.at[0, :, pl.ds(pl.multiple_of(others[t] * 2 * rows, LANES), 2 * rows)],
            dst_ref=xbuf.at[chip], send_sem=x_ss.at[t], recv_sem=x_rs.at[t],
            device_id={"grp": others[t] * 2 + core}, device_id_type=MESH)

    half = cw // 2

    def q_copy(p, way):
        slot, part, to = (
            (chip, pl.ds(0, cw), xn), (chip, pl.ds(0, cw), yn),
            (xn, pl.ds(0, half), yn), (yn, pl.ds(half, half), xn))[way]
        return pltpu.make_async_remote_copy(
            src_ref=dqbuf.at[p, slot, part], dst_ref=dqbuf.at[p, slot, part],
            send_sem=q_ss.at[p, way], recv_sem=q_rs.at[p, way],
            device_id={"grp": to * 2 + core}, device_id_type=MESH)

    def pair_copy(p):
        return pltpu.make_async_remote_copy(
            src_ref=e_send.at[p], dst_ref=e_recv.at[p], send_sem=e_ss.at[p], recv_sem=e_rs.at[p],
            device_id={"grp": chip * 2 + 1 - core}, device_id_type=MESH)

    side = lax.rem(c, 2)
    near, far = c + 1 - 2 * side, lax.rem(c + 2, n)
    hw = cw // 2

    def near_copy(p):
        return pltpu.make_async_remote_copy(
            src_ref=r_send.at[p], dst_ref=r_recv.at[p], send_sem=r_ss.at[p], recv_sem=r_rs.at[p],
            device_id={"ctx": near}, device_id_type=MESH)

    def far_copy(p):
        return pltpu.make_async_remote_copy(
            src_ref=f_send.at[p], dst_ref=f_recv.at[p], send_sem=f_ss.at[p], recv_sem=f_rs.at[p],
            device_id={"ctx": far}, device_id_type=MESH)

    def sum_copy(p):
        return pltpu.make_async_remote_copy(
            src_ref=a_send.at[p], dst_ref=a_recv.at[p], send_sem=a_ss.at[p], recv_sem=a_rs.at[p],
            device_id={"ctx": near}, device_id_type=MESH)

    def part_copy(t):
        owner = lax.rem(c + n - t, n)
        return pltpu.make_async_remote_copy(
            src_ref=kv_send.at[owner], dst_ref=kv_recv.at[t - 1],
            send_sem=p_ss.at[t - 1], recv_sem=p_rs.at[t - 1],
            device_id={"ctx": owner}, device_id_type=MESH)

    pl.semaphore_wait(barrier, n - 1 + chips)
    for t in range(n - 1, 0, -1):
        @pl.when(c + t < n)
        def _():
            for copy in key_copy(t):
                copy.start()
    for t in range(3):
        x_copy(t).start()

    loads[0].wait()
    lane = lax.broadcasted_iota(jnp.int32, (tok, tok), 1)
    sub = lax.broadcasted_iota(jnp.int32, (tok, tok), 0)
    q_seg = seg_ref[:, pl.ds(pl.multiple_of(c * tok, LANES), tok)]

    def make_bias(j, _):
        k_seg = seg_ref[:, pl.ds(pl.multiple_of(j * tok, LANES), tok)]
        k_cols = jnp.transpose(jnp.broadcast_to(k_seg, (tok, tok)).astype(f32))
        same = k_cols == jnp.broadcast_to(q_seg, (tok, tok)).astype(f32)
        bias[j] = jnp.where(same & (j * tok + sub <= c * tok + lane), 0.0, HIDDEN)
        return 0

    lax.fori_loop(0, c + 1, make_bias, 0)

    for load in loads[1:4]:
        load.wait()
    head = lax.broadcasted_iota(jnp.int32, (heads, heads * hd), 0)
    column = lax.broadcasted_iota(jnp.int32, (heads, heads * hd), 1)
    pick = jnp.where(column // hd == head, 1.0, 0.0).astype(bf)
    terms = g_ref[0].astype(f32) * f_ref[0].astype(f32)
    high = terms.astype(bf)
    low = (terms - high.astype(f32)).astype(bf)
    delta[...] = dot(pick, high, NT) + dot(pick, low, NT)

    for load in loads[4:7]:
        load.wait()

    def stack(ref, p):
        return jnp.concatenate(
            [ref[0, :, pl.ds(pl.multiple_of(p * cw + i * hd, LANES), hd)] for i in range(hp)], axis=0)

    def row(load, p):
        return jnp.concatenate([load(p * hp + i) for i in range(hp)], axis=1)

    def tiles(p, k, v, hide):
        qs, gs = stack(q_ref, p), stack(g_ref, p)
        lse_row = row(lambda h: lse_ref[0, pl.ds(h, 1), :], p)
        delta_row = row(lambda h: delta[pl.ds(h, 1), :], p)
        hide = jnp.concatenate([hide] * hp, axis=1)
        probs = jnp.exp(dot(k, qs, NT) * scale - lse_row + hide)
        ds = (probs * (dot(v, gs, NT) - delta_row)).astype(bf)
        return ds, dot(probs.astype(bf), gs), dot(ds, qs)

    def finish(p, dqt):
        dqt = (dqt * scale).astype(bf)
        for i in range(hp):
            dqbuf[p, chip, i * hd:(i + 1) * hd] = dqt[:, i * tok:(i + 1) * tok]

        @pl.when(p > n - 1 - AHEAD)
        def _():
            q_copy(p, 0).start()
            q_copy(p, 1).start()

    def turn(block):
        return jnp.transpose(block.astype(f32)).astype(bf)

    kt[c] = turn(kbuf[c])
    dk_acc[c] = jnp.zeros((tok, hd), f32)
    dv_acc[c] = jnp.zeros((tok, hd), f32)

    def diagonal(i, last):
        p = n - 1 - i
        ds, dv, dk = tiles(p, kbuf[c], vbuf[c], bias[c])
        dv_acc[c] += dv
        dk_acc[c] += dk
        dqt = dot(kt[c], ds)
        if last:
            finish(p, dqt)
        else:
            dqt_acc[p] = dqt
        return 0

    def earlier(count):
        for j in range(count - 1, -1, -1):
            for copy in key_arrival(j):
                copy.wait_recv()
            kt[j] = turn(kbuf[j])
            dk_acc[j] = jnp.zeros((tok, hd), f32)
            dv_acc[j] = jnp.zeros((tok, hd), f32)

        def chunk(i, _):
            p = n - 1 - i
            ds, dv, dk = tiles(
                p, kbuf[:count].reshape(count * tok, hd), vbuf[:count].reshape(count * tok, hd),
                bias[:count].reshape(count * tok, tok))
            dqt = dqt_acc[p] + dot(jnp.concatenate([kt[j] for j in range(count)], axis=1), ds)
            finish(p, dqt)
            dv_acc[:count] += dv.reshape(count, tok, hd)
            dk_acc[:count] += dk.reshape(count, tok, hd)
            return 0

        lax.fori_loop(0, n, chunk, 0)
        for j in range(count):
            kv_send[j, 0] = (dk_acc[j] * scale).astype(bf)
            kv_send[j, 1] = dv_acc[j].astype(bf)
        for t in range(1, count + 1):
            part_copy(t).start()

    @pl.when(c == 0)
    def _():
        lax.fori_loop(0, n, lambda i, _: diagonal(i, True), 0)

    @pl.when(c > 0)
    def _():
        lax.fori_loop(0, n, lambda i, _: diagonal(i, False), 0)

    for count in range(1, n):
        @pl.when(c == count)
        def _():
            earlier(count)

    loads[7].wait()
    for t in range(3):
        x_copy(t).wait_recv()
    for s in range(chips):
        for i in range(2):
            which = lax.rem(core + i, 2)
            xt[i * rows:(i + 1) * rows, s * tok:(s + 1) * tok] = turn(
                xbuf[s, :, pl.ds(pl.multiple_of(which * rows, LANES), rows)])

    def gather_parts():
        dk_acc[c] = dk_acc[c] * scale
        for t in range(1, n):
            @pl.when(c + t < n)
            def _():
                part_copy(t).wait_recv()
                dk_acc[c] += kv_recv[t - 1, 0].astype(f32)
                dv_acc[c] += kv_recv[t - 1, 1].astype(f32)
        dk_ref[0] = dk_acc[c].astype(bf)
        dv_ref[0] = dv_acc[c].astype(bf)

    def forward(p):
        for way in range(2):
            q_copy(p, way).wait_recv()
            q_copy(p, way + 2).start()
        if p >= AHEAD:
            q_copy(p - AHEAD, 0).start()
            q_copy(p - AHEAD, 1).start()

    def multiply(p):
        for way in (2, 3):
            q_copy(p, way).wait_recv()
        product = dot(xt[...], jnp.concatenate([dqbuf[p, s] for s in range(chips)], axis=1), NT)
        e_send[p] = product[rows:].astype(bf)
        pair_copy(p).start()
        own[p] = product[:rows]
        for i in range(hp):
            dq_ref[0, :, p * cw + i * hd:p * cw + (i + 1) * hd] = turn(dqbuf[p, chip, i * hd:(i + 1) * hd])

    def exchange(p):
        pair_copy(p).wait_recv()
        own[p] += e_recv[p].astype(f32)
        r_send[p] = own[p, :, pl.ds(pl.multiple_of((1 - side) * hw, LANES), hw)].astype(bf)
        near_copy(p).start()

    def across(p):
        near_copy(p).wait_recv()
        total = own[p, :, pl.ds(pl.multiple_of(side * hw, LANES), hw)] + r_recv[p].astype(f32)
        f_send[p] = total.astype(bf)
        far_copy(p).start()

    def settle(p):
        far_copy(p).wait_recv()
        a_send[p] = (f_send[p].astype(f32) + f_recv[p].astype(f32)).astype(bf)
        sum_copy(p).start()
        gw_ref[:, pl.ds(pl.multiple_of(p * cw + side * hw, LANES), hw)] = a_send[p].astype(f32)

    def collect(p):
        sum_copy(p).wait_recv()
        gw_ref[:, pl.ds(pl.multiple_of(p * cw + (1 - side) * hw, LANES), hw)] = a_recv[p].astype(f32)

    forward(n - 1 - 0)
    forward(n - 1 - 1)
    multiply(n - 1 - 0)
    exchange(n - 1 - 0)
    forward(n - 1 - 2)
    multiply(n - 1 - 1)
    exchange(n - 1 - 1)
    forward(n - 1 - 3)
    multiply(n - 1 - 2)
    exchange(n - 1 - 2)
    across(n - 1 - 0)
    multiply(n - 1 - 3)
    exchange(n - 1 - 3)
    across(n - 1 - 1)
    across(n - 1 - 2)
    settle(n - 1 - 0)
    across(n - 1 - 3)
    settle(n - 1 - 1)
    settle(n - 1 - 2)
    settle(n - 1 - 3)
    collect(n - 1 - 0)
    collect(n - 1 - 1)
    collect(n - 1 - 2)
    collect(n - 1 - 3)
    gather_parts()

    for t in range(1, n):
        @pl.when(c + t < n)
        def _():
            for copy in key_copy(t):
                copy.wait_send()

        @pl.when(c >= t)
        def _():
            part_copy(t).wait_send()
    for t in range(3):
        x_copy(t).wait_send()
    for p in range(n):
        for way in range(4):
            q_copy(p, way).wait_send()
        for copy in (pair_copy(p), near_copy(p), far_copy(p), sum_copy(p)):
            copy.wait_send()


def store(*refs):
    sources, targets, sem = refs[:4], refs[4:8], refs[8]
    copies = [pltpu.make_async_copy(a, b, sem.at[i]) for i, (a, b) in enumerate(zip(sources, targets))]
    for copy in copies:
        copy.start()
    for copy in copies:
        copy.wait()


def fused(n, grp, queries, keys, values, d_out, fwd_out, lse, segment_ids, layer_input):
    tok, hd, heads = keys.shape[1], keys.shape[2], lse.shape[1]
    width, rows = queries.shape[2], layer_input.shape[2] // grp
    chips, cw = grp // 2, width // n
    bf, f32 = jnp.bfloat16, jnp.float32
    dma = pltpu.SemaphoreType.DMA
    vmem = pl.BlockSpec(memory_space=pltpu.VMEM)
    hbm = pl.BlockSpec(memory_space=pl.ANY)
    shapes = (
        jax.ShapeDtypeStruct((1, tok, width), bf),
        jax.ShapeDtypeStruct((1, tok, hd), bf),
        jax.ShapeDtypeStruct((1, tok, hd), bf),
        jax.ShapeDtypeStruct((rows, width), f32),
    )
    inputs = (queries, keys, values, d_out, fwd_out, lse, segment_ids, layer_input)
    results = pl.pallas_call(
        functools.partial(kernel, n, grp, heads),
        out_shape=shapes,
        in_specs=[hbm] * 8,
        out_specs=(vmem,) * 4,
        scratch_shapes=[
            pltpu.VMEM((1, heads, tok), f32), pltpu.VMEM((1, tok * n), jnp.int32),
            pltpu.VMEM((1, tok, width), bf), pltpu.VMEM((1, tok, width), bf), pltpu.VMEM((1, tok, width), bf),
            pltpu.VMEM((n, tok, hd), bf), pltpu.VMEM((n, tok, hd), bf),
            pltpu.VMEM((chips, tok, 2 * rows), bf), dma((8,)),
            pltpu.VMEM((n, tok, tok), f32), pltpu.VMEM((heads, tok), f32),
            pltpu.VMEM((n, hd, tok), bf), pltpu.VMEM((2 * rows, chips * tok), bf),
            pltpu.VMEM((n, tok, hd), f32), pltpu.VMEM((n, tok, hd), f32),
            pltpu.VMEM((n, hd, cw), f32), pltpu.VMEM((n, chips, cw, tok), bf),
            pltpu.VMEM((n, rows, cw), f32),
            pltpu.VMEM((n, rows, cw), bf), pltpu.VMEM((n, rows, cw), bf),
            *[pltpu.VMEM((n, rows, cw // 2), bf)] * 6,
            pltpu.VMEM((n, 2, tok, hd), bf), pltpu.VMEM((n - 1, 2, tok, hd), bf),
            dma((n - 1,)), dma((n - 1,)), dma((n,)), dma((n,)),
            dma((3,)), dma((3,)), dma((n, 4)), dma((n, 4)), dma((n,)), dma((n,)),
            *[dma((n,))] * 6, dma((n - 1,)), dma((n - 1,)),
        ],
        compiler_params=pltpu.CompilerParams(collective_id=0, has_side_effects=True, vmem_limit_bytes=24 << 20),
    )(*[pltpu.with_memory_space_constraint(a, pltpu.HBM) for a in inputs])
    return pl.pallas_call(
        store,
        out_shape=shapes,
        in_specs=[vmem] * 4,
        out_specs=(hbm,) * 4,
        scratch_shapes=[dma((4,))],
        compiler_params=pltpu.CompilerParams(vmem_limit_bytes=8 << 20),
    )(*results)


def on_device(queries, keys, values, d_out, fwd_out, lse, segment_ids, layer_input):
    tok = queries.shape[1]
    heads = lse.shape[1]
    head_dim = keys.shape[2]
    scale = head_dim ** (-0.5)
    seg_all = segment_ids[0]
    q_start = lax.axis_index("ctx") * tok
    q_heads = queries[0].reshape(tok, heads, head_dim)
    grad_heads = d_out[0].reshape(tok, heads, head_dim)
    delta = jnp.sum(
        grad_heads.astype(jnp.float32)
        * fwd_out[0].reshape(tok, heads, head_dim).astype(jnp.float32),
        axis=2,
    )
    delta_rows = jnp.transpose(delta)
    lse_rows = lse[0]
    q_seg = lax.dynamic_slice_in_dim(seg_all, q_start, tok, 0)
    q_pos = q_start + jnp.arange(tok, dtype=jnp.int32)
    key_rows = lax.all_gather(keys, "ctx", axis=1, tiled=True)[0]
    value_rows = lax.all_gather(values, "ctx", axis=1, tiled=True)[0]
    count = key_rows.shape[0]
    k_pos = jnp.arange(count, dtype=jnp.int32)
    visible = (q_seg[:, None] == seg_all[None, :]) & (k_pos[None, :] <= q_pos[:, None])
    scores = (
        jnp.einsum("qhd,kd->hqk", q_heads, key_rows, preferred_element_type=jnp.float32) * scale
    )
    probs = jnp.where(visible[None], jnp.exp(scores - lse_rows[:, :, None]), 0.0)
    probs_b = probs.astype(jnp.bfloat16)
    dprobs = jnp.einsum("qhd,kd->hqk", grad_heads, value_rows, preferred_element_type=jnp.float32)
    dscores = (probs * (dprobs - delta_rows[:, :, None])).astype(jnp.bfloat16)
    dq_acc = (
        jnp.einsum("hqk,kd->qhd", dscores, key_rows, preferred_element_type=jnp.float32) * scale
    )
    grad_k = jnp.einsum("hqk,qhd->kd", dscores, q_heads, preferred_element_type=jnp.float32) * scale
    grad_v = jnp.einsum("hqk,qhd->kd", probs_b, grad_heads, preferred_element_type=jnp.float32)
    block = jnp.concatenate([grad_k, grad_v], axis=1)
    dkv_acc = block
    dq_acc, dkv_acc = (dq_acc, dkv_acc)
    grad_q = dq_acc.reshape(tok, heads * head_dim).astype(jnp.bfloat16)
    owned = lax.psum_scatter(
        dkv_acc.astype(jnp.bfloat16), "ctx", scatter_dimension=0, tiled=True
    ).astype(jnp.float32)
    grad_k = owned[:, :head_dim].astype(jnp.bfloat16)
    grad_v = owned[:, head_dim:].astype(jnp.bfloat16)
    inputs = layer_input[0]
    rows_part = lax.psum_scatter(
        lax.dot_general(
            inputs, grad_q, (((0,), (0,)), ((), ())), preferred_element_type=jnp.float32
        ),
        "grp",
        scatter_dimension=0,
        tiled=True,
    )
    grad_weight = lax.psum(rows_part.astype(jnp.bfloat16), "ctx").astype(jnp.float32)
    return (grad_q[None], grad_k[None], grad_v[None], grad_weight)


def solution(mesh):
    n, grp = mesh.shape["ctx"], mesh.shape["grp"]

    def either(*args):
        tok, depth = args[7].shape[1], args[7].shape[2]
        heads, hd = args[5].shape[1], args[1].shape[2]
        gather = grp == 8 and n == 4 and grp * tok <= depth
        tiled = (depth // grp) % LANES == 0 and tok % LANES == 0 and hd == tok and heads % (2 * n) == 0
        return fused(n, grp, *args) if gather and tiled and heads <= tok else on_device(*args)

    return jax.shard_map(
        either,
        mesh=mesh,
        in_specs=(
            P("grp", "ctx", None),
            P("grp", "ctx", None),
            P("grp", "ctx", None),
            P("grp", "ctx", None),
            P("grp", "ctx", None),
            P("grp", None, "ctx"),
            P("grp", None),
            P("grp", "ctx", None),
        ),
        out_specs=(
            P("grp", "ctx", None),
            P("grp", "ctx", None),
            P("grp", "ctx", None),
            P("grp", None),
        ),
        check_vma=False,
    )
```
